512 devices in a mesh: tm: 16 (over x, y_hi), chan: 32 (over y_lo, z, core).
Axes of the slice: x: 4, y: 8 (y_hi: 4, y_lo: 2; y = y_hi * 2 + y_lo), z: 8, core: 2. Of those that a mesh axis runs over, the one named last changes fastest.
Arguments:
- latent_input: bfloat16 [2048, 1280], P('chan', 'tm'), may hold values from -6 to 6
- upsample_kernel: bfloat16 [16, 1024, 2048], P(None, 'chan', 'tm'), may hold values from -0.09375 to 0.09375
- dilated_kernel: bfloat16 [2, 7, 1024, 1024], P(None, None, 'chan'), may hold values from -0.0625 to 0.0625
- pointwise_kernel: bfloat16 [2, 1024, 1024], P(None, 'chan'), may hold values from -0.1875 to 0.1875
- dilated_prune_mask: int32 [2, 7, 1024, 128], P(None, None, 'chan'), may hold values 0 or 1
- pointwise_prune_mask: int32 [2, 1024, 128], P(None, 'chan'), may hold values 0 or 1
- snake_freq_upsample: float32 [2048], P('chan'), may hold values from 0.5 to 3
- snake_freq_dilated: float32 [2, 1024], P(None, 'chan'), may hold values from 0.5 to 3
- snake_freq_pointwise: float32 [2, 1024], P(None, 'chan'), may hold values from 0.5 to 3
- segment_lengths: int32 [3], replicated, may hold values from 1 to 720, as said below
- cotangent: bfloat16 [1024, 10240], P('chan', 'tm'), may hold values from -6 to 6
Outputs:
- decoded: bfloat16 [1024, 10240], P('chan', 'tm')
- dil_saliency: float32 [2, 7, 1024, 1024], P(None, None, 'chan')
- point_saliency: float32 [2, 1024, 1024], P(None, 'chan')
The draws below stay inside these ranges and needn't reach their ends.
Inputs may be any that keep to these rules, and one draw needn't show every extreme that they name: `segment_lengths`: 3 lengths in latent frames that sum to 1280, in an order drawn with them; the longest is exactly 720.
All inputs are finite; a program needn't handle non-finite values. No bound on the sum of `dilated_prune_mask` or of `pointwise_prune_mask` on one device may be relied on, other than what follows from the above.
Results may differ from the reference program's by a relative error of at most 0.035.
Values may be sent and summed in bfloat16 or wider, within the bound.
No kernel may reach another device: no remote copies, remote signals or barrier semaphores. Data moves between devices by JAX's collectives and lax.ppermute only.
A program may use at most 128 MiB of HBM per device.

```python
import math
import jax
import jax.numpy as jnp
from jax import lax

D_IN = 2048
OUTPUT_CHANNELS = 1024
STRIDE = 8
KT = 16
DILATED_TAPS = 7
RESIDUAL_COUNT = 2
PRUNE_CHANNELS = 8
FR_DEV = 80
FRAMES = 1280
ROWS = 10240
N_CHAN = 32


def draw_segment_lengths(key, part):
    longest = FRAMES // 2 + FR_DEV
    length_key = jax.random.fold_in(key, 11)
    order_key = jax.random.fold_in(key, 23)
    first_length = jax.random.randint(length_key, (), 1, FRAMES // 2 - FR_DEV, dtype=jnp.int32)
    middle_length = jnp.zeros((), jnp.int32) + longest
    last_length = FRAMES - longest - first_length
    lengths = jnp.stack([first_length, middle_length, last_length]).astype(jnp.int32)
    order = jax.random.permutation(order_key, 3)
    return lengths[order].astype(jnp.int32)


def place_ends(drawn, stream_key, low, largest):
    dims = drawn.shape
    place = [jax.random.randint(jax.random.fold_in(stream_key, axis), (), 0, dims[axis]) for axis in range(len(dims))]
    drawn = drawn.at[tuple(place)].set(low)
    longest = dims.index(max(dims))
    place[longest] = (place[longest] + 1) % dims[longest]
    return drawn.at[tuple(place)].set(largest)


def levels(key, dims, pieces, low, largest):
    level = 1.0
    for position, shards_of in pieces:
        steps = jax.random.uniform(jax.random.fold_in(jax.random.fold_in(key, 6), position), (shards_of,), jnp.float32, low / len(pieces), largest / len(pieces))
        level = level * jnp.repeat(jnp.exp(steps), dims[position] // shards_of).reshape((-1,) + (1,) * (len(dims) - 1 - position))
    return level


def noise(stream_key, shape, spread, reach, pieces=(), kind=jnp.bfloat16):
    level = levels(stream_key, shape, pieces, -0.22, 0.18) if pieces else 1.0
    entries = jax.random.normal(stream_key, shape, jnp.float32) * spread * level
    return jnp.minimum(jnp.maximum(entries, -reach), reach).astype(kind)


def setup_inputs(seed: int = 0) -> dict:
    key_of = jax.random.split(jax.random.key(seed), 12)
    latent_input = noise(key_of[0], (D_IN, FRAMES), 1.0, 6.0, ((0, 32), (1, 16)))
    upsample_kernel = noise(key_of[1], (KT, OUTPUT_CHANNELS, D_IN), (2 * D_IN) ** -0.5, 0.09375, ((1, 32), (2, 16)))
    dilated_kernel = noise(key_of[2], (RESIDUAL_COUNT, DILATED_TAPS, OUTPUT_CHANNELS, OUTPUT_CHANNELS), (DILATED_TAPS * OUTPUT_CHANNELS) ** -0.5, 0.0625, ((2, 32),))
    pointwise_kernel = noise(key_of[3], (RESIDUAL_COUNT, OUTPUT_CHANNELS, OUTPUT_CHANNELS), OUTPUT_CHANNELS ** -0.5, 0.1875, ((1, 32),))
    dilated_prune_mask = place_ends((jax.random.randint(key_of[4], (RESIDUAL_COUNT, DILATED_TAPS, OUTPUT_CHANNELS, OUTPUT_CHANNELS // PRUNE_CHANNELS), 0, 4) < 3).astype(jnp.int32), jax.random.fold_in(key_of[4], 1), 0, 1)
    pointwise_prune_mask = place_ends((jax.random.randint(key_of[5], (RESIDUAL_COUNT, OUTPUT_CHANNELS, OUTPUT_CHANNELS // PRUNE_CHANNELS), 0, 4) < 3).astype(jnp.int32), jax.random.fold_in(key_of[5], 1), 0, 1)
    snake_freq_upsample = jnp.clip(jnp.exp(math.log(3.0) - 1.7917595 * jax.random.uniform(key_of[6], (D_IN,), jnp.float32) ** levels(key_of[6], (D_IN,), ((0, 32),), -0.2, 0.2)), 0.5, 3.0)
    snake_freq_dilated = jnp.clip(jnp.exp(math.log(3.0) - 1.7917595 * jax.random.uniform(key_of[7], (RESIDUAL_COUNT, OUTPUT_CHANNELS), jnp.float32) ** levels(key_of[7], (RESIDUAL_COUNT, OUTPUT_CHANNELS), ((1, 32),), -0.2, 0.2)), 0.5, 3.0)
    snake_freq_pointwise = jnp.clip(jnp.exp(math.log(3.0) - 1.7917595 * jax.random.uniform(key_of[8], (RESIDUAL_COUNT, OUTPUT_CHANNELS), jnp.float32) ** levels(key_of[8], (RESIDUAL_COUNT, OUTPUT_CHANNELS), ((1, 32),), -0.2, 0.2)), 0.5, 3.0)
    segment_lengths = draw_segment_lengths(jax.random.fold_in(key_of[11], 71), 0)
    cotangent = noise(key_of[10], (OUTPUT_CHANNELS, ROWS), 1.0, 6.0, ((0, 32), (1, 16)))
    return {"latent_input": latent_input, "upsample_kernel": upsample_kernel, "dilated_kernel": dilated_kernel, "pointwise_kernel": pointwise_kernel, "dilated_prune_mask": dilated_prune_mask, "pointwise_prune_mask": pointwise_prune_mask, "snake_freq_upsample": snake_freq_upsample, "snake_freq_dilated": snake_freq_dilated, "snake_freq_pointwise": snake_freq_pointwise, "segment_lengths": segment_lengths, "cotangent": cotangent}


def snake_act(values, alpha):
    scale = alpha[:, None]
    return values + jnp.sin(scale * values) ** 2 / scale


def snake_slope(values, alpha):
    return 1.0 + jnp.sin(2.0 * alpha[:, None] * values)


def track_ids(lengths, frame_index, total_frames):
    starts = jnp.cumsum(lengths) - lengths
    found = jnp.sum((starts[:, None] <= frame_index[None, :]).astype(jnp.int32), axis=0) - 1
    return jnp.where(frame_index < 0, -1, jnp.where(frame_index >= total_frames, -2, found)).astype(jnp.int32)


def rounded_groups(grouped_weight_sums, grad_groups, contract):
    def step_fn(totals, inputs):
        weight_part, grad_part = inputs
        partial_sum = lax.dot_general(weight_part, grad_part, ((contract, contract), ((), ())), preferred_element_type=jnp.float32)
        narrow = lax.optimization_barrier(partial_sum.astype(jnp.bfloat16))
        return totals + narrow.astype(jnp.float32), None

    start_sum = jnp.zeros((grouped_weight_sums.shape[-1], grad_groups.shape[-1]), jnp.float32)
    result, unused = lax.scan(step_fn, start_sum, (grouped_weight_sums, grad_groups))
    return result


def reference(latent_input, upsample_kernel, dilated_kernel, pointwise_kernel, dilated_prune_mask, pointwise_prune_mask, snake_freq_upsample, snake_freq_dilated, snake_freq_pointwise, segment_lengths, cotangent):
    half_stride = STRIDE // 2
    channel_group_width = OUTPUT_CHANNELS // N_CHAN
    frame_pos = jnp.arange(FRAMES, dtype=jnp.int32)
    activated = snake_act(latent_input.astype(jnp.float32), snake_freq_upsample).astype(jnp.bfloat16)
    frame_ids = track_ids(segment_lengths, frame_pos, FRAMES)
    prev_ok = (frame_ids == track_ids(segment_lengths, frame_pos - 1, FRAMES)).astype(jnp.float32)
    next_ok = (frame_ids == track_ids(segment_lengths, frame_pos + 1, FRAMES)).astype(jnp.float32)
    zero_column = jnp.zeros((D_IN, 1), jnp.bfloat16)
    earlier = jnp.concatenate([zero_column, activated[:, :-1]], axis=1)
    later = jnp.concatenate([activated[:, 1:], zero_column], axis=1)
    outputs = []
    for phase_index in range(STRIDE):
        middle = jnp.dot(upsample_kernel[phase_index + half_stride], activated, preferred_element_type=jnp.float32)
        if phase_index < half_stride:
            neighbour = jnp.dot(upsample_kernel[phase_index + half_stride + STRIDE], earlier, preferred_element_type=jnp.float32) * prev_ok[None, :]
        else:
            neighbour = jnp.dot(upsample_kernel[phase_index - half_stride], later, preferred_element_type=jnp.float32) * next_ok[None, :]
        outputs.append(middle + neighbour)
    hidden_state = jnp.stack(outputs, axis=-1).reshape(OUTPUT_CHANNELS, ROWS)

    row_pos = jnp.arange(ROWS, dtype=jnp.int32)
    own_ids = track_ids(segment_lengths, jnp.floor_divide(row_pos, STRIDE), FRAMES)

    def tap_mask(offset):
        other = track_ids(segment_lengths, jnp.floor_divide(row_pos + offset, STRIDE), FRAMES)
        return (own_ids == other).astype(jnp.float32)

    saved_residuals = []
    for residual_unit_index in range(RESIDUAL_COUNT):
        spacing = 3 ** (residual_unit_index + 1)
        margin = 3 * spacing
        dilated_effective = dilated_kernel[residual_unit_index] * jnp.repeat(dilated_prune_mask[residual_unit_index], PRUNE_CHANNELS, axis=-1).astype(jnp.bfloat16)
        pointwise_effective = pointwise_kernel[residual_unit_index] * jnp.repeat(pointwise_prune_mask[residual_unit_index], PRUNE_CHANNELS, axis=-1).astype(jnp.bfloat16)
        first = snake_act(hidden_state, snake_freq_dilated[residual_unit_index]).astype(jnp.bfloat16)
        padded_input = jnp.pad(first, ((0, 0), (margin, margin)))
        kernel_tap_masks = jnp.stack([tap_mask((kernel_tap_index - 3) * spacing) for kernel_tap_index in range(DILATED_TAPS)])
        conv_result = jnp.zeros((OUTPUT_CHANNELS, ROWS), jnp.float32)
        for kernel_tap_index in range(DILATED_TAPS):
            track_window = padded_input[:, kernel_tap_index * spacing:kernel_tap_index * spacing + ROWS]
            conv_result = conv_result + kernel_tap_masks[kernel_tap_index][None, :] * jnp.dot(dilated_effective[kernel_tap_index], track_window, preferred_element_type=jnp.float32)
        second_activation = snake_act(conv_result, snake_freq_pointwise[residual_unit_index]).astype(jnp.bfloat16)
        saved_residuals.append((hidden_state, padded_input, kernel_tap_masks, conv_result, second_activation, dilated_effective, pointwise_effective))
        hidden_state = hidden_state + jnp.dot(pointwise_effective, second_activation, preferred_element_type=jnp.float32)
    decoded = hidden_state.astype(jnp.bfloat16)

    grad_out = cotangent.astype(jnp.float32)
    dilated_weight_list = [None] * RESIDUAL_COUNT
    pointwise_weight_list = [None] * RESIDUAL_COUNT
    for residual_unit_index in reversed(range(RESIDUAL_COUNT)):
        spacing = 3 ** (residual_unit_index + 1)
        margin = 3 * spacing
        hidden_input, padded_input, kernel_tap_masks, conv_result, second_activation, dilated_effective, pointwise_effective = saved_residuals[residual_unit_index]
        grad_b = grad_out.astype(jnp.bfloat16)
        pointwise_gradient = lax.dot_general(grad_b, second_activation, (((1,), (1,)), ((), ())), preferred_element_type=jnp.float32)
        grad_second = rounded_groups(pointwise_effective.reshape(N_CHAN, channel_group_width, OUTPUT_CHANNELS), grad_b.reshape(N_CHAN, channel_group_width, ROWS), (0,))
        grad_conv = (grad_second * snake_slope(conv_result, snake_freq_pointwise[residual_unit_index])).astype(jnp.bfloat16)
        masked_kernel = grad_conv[None, :, :] * kernel_tap_masks[:, None, :].astype(jnp.bfloat16)
        track_window_list = jnp.stack([padded_input[:, kernel_tap_index * spacing:kernel_tap_index * spacing + ROWS] for kernel_tap_index in range(DILATED_TAPS)])
        dilated_gradient = jnp.einsum("jdo,jso->jds", masked_kernel.astype(jnp.float32), track_window_list.astype(jnp.float32))
        dilated_weight_list[residual_unit_index] = dilated_effective.astype(jnp.float32) * dilated_gradient
        pointwise_weight_list[residual_unit_index] = pointwise_effective.astype(jnp.float32) * pointwise_gradient
        if residual_unit_index > 0:
            shifted_pad = jnp.pad(masked_kernel, ((0, 0), (0, 0), (margin, margin)))
            shifted = jnp.stack([shifted_pad[kernel_tap_index, :, (6 - kernel_tap_index) * spacing:(6 - kernel_tap_index) * spacing + ROWS] for kernel_tap_index in range(DILATED_TAPS)])
            grouped_weight_sums = dilated_effective.reshape(DILATED_TAPS, N_CHAN, channel_group_width, OUTPUT_CHANNELS).transpose(1, 0, 2, 3)
            grad_groups = shifted.reshape(DILATED_TAPS, N_CHAN, channel_group_width, ROWS).transpose(1, 0, 2, 3)
            grad_first = rounded_groups(grouped_weight_sums, grad_groups, (0, 1))
            grad_out = grad_out + grad_first * snake_slope(hidden_input, snake_freq_dilated[residual_unit_index])
    return decoded, jnp.stack(dilated_weight_list), jnp.stack(pointwise_weight_list)
```

```python
import jax
import jax.numpy as jnp
from jax import lax
from jax.sharding import Mesh, PartitionSpec as P

TM = ("x", "yh")
CHAN = ("yl", "z", "k")
QUAD = ("yl", "k")
SLOT = ("x", "yh", "yl", "k")
EDGE_FRAMES = 5
EXT_UP = 40
EXT_MID = 28
EXT_GRAD = 40
EXT_BACK = 12
f32 = jnp.float32
bf16 = jnp.bfloat16


def exchange(pieces, axes):
    return lax.all_to_all(pieces, axes, 0, 0, tiled=True)


def copies(value, axes):
    size = lax.axis_size(axes)
    return exchange(jnp.broadcast_to(value[None], (size, *value.shape)), axes)


def shift_pairs(axes, step):
    size = lax.axis_size(axes)
    return [(i, i + step) for i in range(size) if 0 <= i + step < size]


def from_before(value, axes):
    return lax.ppermute(value, axes, shift_pairs(axes, 1))


def from_after(value, axes):
    return lax.ppermute(value, axes, shift_pairs(axes, -1))


def snake_act(values, alpha):
    return values + jnp.sin(alpha * values) ** 2 / alpha


def snake_slope(values, alpha):
    return 1.0 + jnp.sin(2.0 * alpha * values)


def all_channels(blocks):
    return blocks.transpose(1, 0, 2).reshape(blocks.shape[1], -1)


def per_device(
    latent_input,
    upsample_kernel,
    dilated_kernel,
    pointwise_kernel,
    dilated_prune_mask,
    pointwise_prune_mask,
    snake_freq_upsample,
    snake_freq_dilated,
    snake_freq_pointwise,
    segment_lengths,
    cotangent,
):
    taps2, width, cols = upsample_kernel.shape
    stride = taps2 // 2
    frames = latent_input.shape[1]
    tm_size = lax.axis_size(TM)
    quad = lax.axis_size(QUAD)
    z_size = lax.axis_size("z")
    y_size = lax.axis_size("yl")
    total_frames = frames * tm_size
    slot_latent = frames // quad
    slot = slot_latent * stride
    units, taps, _, channels = dilated_kernel.shape
    block = quad * width
    tm_index = lax.axis_index(TM)
    slot_start = (tm_index * quad + lax.axis_index(QUAD)) * slot

    starts = jnp.cumsum(segment_lengths) - segment_lengths

    def ids_of(latent_frame):
        found = jnp.sum((starts[:, None] <= latent_frame[None, :]).astype(jnp.int32), axis=0) - 1
        return jnp.where(
            latent_frame < 0, -1, jnp.where(latent_frame >= total_frames, -2, found)
        )

    def tap_masks(extent, spacing, sign, start):
        rows = start + jnp.arange(-extent, slot + extent, dtype=jnp.int32)
        own = ids_of(jnp.floor_divide(rows, stride))
        return [
            own == ids_of(jnp.floor_divide(rows + sign * (tap - 3) * spacing, stride))
            for tap in range(taps)
        ]

    def pruned(kernel, mask):
        lanes = mask.shape[-1]
        group = jnp.arange(channels, dtype=jnp.int32) // (channels // lanes)
        expand = (jnp.arange(lanes, dtype=jnp.int32)[:, None] == group[None, :]).astype(bf16)
        rows = mask.astype(bf16).reshape(-1, lanes)
        wide_mask = jnp.dot(rows, expand, preferred_element_type=f32).astype(bf16)
        return (kernel.reshape(-1, channels) * wide_mask).reshape(kernel.shape)

    lane = jnp.arange(channels, dtype=jnp.int32)
    part = channels // (z_size * y_size)
    source = (lane // part) % y_size * (z_size * part) + lane // (y_size * part) * part + lane % part
    reorder = (lane[:, None] == source[None, :]).astype(bf16)

    def z_first(value):
        return jnp.dot(value.reshape(-1, channels), reorder, preferred_element_type=f32).astype(bf16).reshape(value.shape)

    def natural(value):
        return lax.dot_general(
            value, reorder, (((1,), (1,)), ((), ())), preferred_element_type=f32
        ).astype(bf16)

    def over_quad(value, axis):
        def spread(value, name, axis):
            both = lax.ppermute(value, name, [(0, 1), (1, 0)])
            pick = (jnp.arange(2, dtype=jnp.int32) == lax.axis_index(name)).reshape(
                (1,) * axis + (2,) + (1,) * (value.ndim - axis)
            )
            return jnp.where(pick, jnp.expand_dims(value, axis), jnp.expand_dims(both, axis))

        out = spread(spread(value, "yl", axis), "k", axis + 1)
        return out.reshape(*value.shape[:axis], quad, *value.shape[axis:])

    x_size = lax.axis_size("x")
    margin = EDGE_FRAMES + 1
    span = frames + 2 * margin
    kernel_yh = copies(upsample_kernel.reshape(taps2 * width, cols), "yh")
    wide = jnp.concatenate(
        [
            from_before(latent_input[:, -margin:], TM),
            latent_input,
            from_after(latent_input[:, :margin], TM),
        ],
        axis=1,
    )
    wide = snake_act(wide.astype(f32), snake_freq_upsample[:, None]).astype(bf16)
    inputs_all = copies(wide, CHAN)
    inputs_x = exchange(inputs_all.reshape(x_size, -1, span), "x")
    inputs_x = inputs_x.reshape(x_size, -1, cols, span)
    mixed = jnp.einsum("xmit,moi->xto", inputs_x, kernel_yh, preferred_element_type=f32)
    half = stride // 2 * width
    wide_latent = slot_latent + 2 * EDGE_FRAMES
    freqs = jnp.concatenate([snake_freq_dilated, snake_freq_pointwise]).reshape(1, -1)
    freqs = jnp.pad(freqs, ((0, 0), (0, stride * width - freqs.shape[1])))
    thirds = []
    for _ in range(3):
        thirds.append(lax.reduce_precision(freqs, 8, 7))
        freqs = freqs - thirds[-1]
    thirds = jnp.concatenate(thirds).astype(bf16)
    pieces = []
    for xi in range(x_size):
        index = xi * lax.axis_size("yh") + lax.axis_index("yh")
        lat = index * frames + jnp.arange(-EDGE_FRAMES, frames + EDGE_FRAMES, dtype=jnp.int32)
        here = ids_of(lat)
        prev_ok = (here == ids_of(lat - 1)).astype(f32)[:, None]
        next_ok = (here == ids_of(lat + 1)).astype(f32)[:, None]
        part = mixed[xi]
        up = jnp.concatenate(
            [
                part[1:-1, half : 2 * half] + prev_ok * part[:-2, 3 * half :],
                part[1:-1, 2 * half : 3 * half] + next_ok * part[2:, :half],
            ],
            axis=1,
        ).astype(bf16)
        for q in range(quad):
            pieces.append(
                jnp.concatenate([up[q * slot_latent : q * slot_latent + wide_latent], thirds])
            )
    arrived = exchange(jnp.stack(pieces), ("x", "yl", "k"))
    arrived = arrived.reshape(x_size, quad, wide_latent + 3, stride * width).astype(f32)
    hidden = (
        arrived[:, :, :wide_latent]
        .sum(axis=0)
        .reshape(quad, wide_latent, stride, width)
        .transpose(1, 2, 0, 3)
        .reshape(wide_latent * stride, block)
    )
    freqs = arrived[0, :, wide_latent:, : 2 * units * width].sum(axis=1)
    freqs = freqs.reshape(quad, 2 * units, width).transpose(1, 0, 2).reshape(2 * units, 1, block)
    freq_dil, freq_point = freqs[:units], freqs[units:]

    dil_eff = pruned(dilated_kernel, dilated_prune_mask)
    point_eff = pruned(pointwise_kernel, pointwise_prune_mask)
    w_point = copies(z_first(point_eff), QUAD)
    w_point = w_point.transpose(1, 0, 2, 3).reshape(units, block, channels)
    dil_z = z_first(dil_eff)
    w_dil = [over_quad(dil_z[u], 1).reshape(taps * block, channels) for u in range(units)]

    cot = exchange(
        cotangent.reshape(width, quad, slot).transpose(1, 0, 2), QUAD
    ).reshape(block, slot).T

    def to_owner(partial):
        rows = partial.shape[0]
        pieces = partial.astype(bf16).reshape(rows, z_size, block).transpose(1, 0, 2)
        return exchange(pieces, "z").astype(f32).sum(axis=0)

    grad_second1 = to_owner(jnp.dot(cot, w_point[1], preferred_element_type=f32))
    hidden, grad_second1 = lax.optimization_barrier((hidden, grad_second1))

    def conv(inputs, weights, masks, first_row, spacing, rows):
        full = lax.dot_general(
            inputs, weights, (((1,), (1,)), ((), ())), preferred_element_type=f32
        )
        total = 0.0
        for tap in range(taps):
            begin = first_row + tap * spacing
            part = full[begin : begin + rows, tap * block : (tap + 1) * block]
            total = total + jnp.where(masks[tap][:, None], part, 0.0)
        return total

    rows0 = slot + 2 * EXT_MID
    first0 = snake_act(hidden, freq_dil[0]).astype(bf16)
    first0_blocks = copies(first0, "z")
    first0_all = all_channels(first0_blocks)
    conv0 = conv(
        first0_all,
        w_dil[0],
        tap_masks(EXT_MID, 3, 1, slot_start),
        EXT_UP - EXT_MID - 9,
        3,
        rows0,
    )
    second0 = snake_act(conv0, freq_point[0]).astype(bf16)
    second0_all = all_channels(copies(second0, "z"))
    gap = EXT_UP - EXT_MID
    hidden1 = hidden[gap : gap + rows0] + lax.dot_general(
        second0_all, w_point[0], (((1,), (1,)), ((), ())), preferred_element_type=f32
    )
    first1 = snake_act(hidden1, freq_dil[1]).astype(bf16)
    first1_blocks = copies(first1, "z")
    first1_all = all_channels(first1_blocks)
    conv1 = conv(
        first1_all,
        w_dil[1],
        tap_masks(0, 9, 1, slot_start),
        EXT_MID - 27,
        9,
        slot,
    )
    second1 = snake_act(conv1, freq_point[1]).astype(bf16)
    second1_all = all_channels(copies(second1, "z"))
    decoded_block = hidden1[EXT_MID : EXT_MID + slot] + lax.dot_general(
        second1_all, w_point[1], (((1,), (1,)), ((), ())), preferred_element_type=f32
    )
    decoded = (
        exchange(decoded_block.astype(bf16).T.reshape(quad, width, slot), QUAD)
        .transpose(1, 0, 2)
        .reshape(width, quad * slot)
    )

    grad_conv1 = (grad_second1 * snake_slope(conv1, freq_point[1])).astype(bf16)
    side = 16
    both = jnp.concatenate([grad_conv1[-EXT_GRAD:], cot[-side:]])
    before = from_before(both, SLOT)
    both = jnp.concatenate([grad_conv1[:EXT_GRAD], cot[:side]])
    after = from_after(both, SLOT)
    grad_conv1 = jnp.concatenate([before[:EXT_GRAD], grad_conv1, after[:EXT_GRAD]])
    cot_wide = jnp.concatenate(
        [before[EXT_GRAD + side - EXT_BACK :], cot, after[EXT_GRAD : EXT_GRAD + EXT_BACK]]
    )
    rows_back = slot + 2 * EXT_BACK
    masks = tap_masks(EXT_BACK, 9, -1, slot_start)
    windows = []
    for tap in range(taps):
        begin = EXT_GRAD - EXT_BACK - 9 * (tap - 3)
        part = grad_conv1[begin : begin + rows_back]
        windows.append(jnp.where(masks[tap][:, None], part, jnp.zeros((), bf16)))
    windows = jnp.concatenate(windows, axis=1)
    grad_first1 = to_owner(jnp.dot(windows, w_dil[1], preferred_element_type=f32))
    skip = EXT_MID - EXT_BACK
    grad_out0 = cot_wide.astype(f32) + grad_first1 * snake_slope(
        hidden1[skip : skip + rows_back], freq_dil[1]
    )
    grad_b0 = grad_out0.astype(bf16)
    grad_second0 = to_owner(jnp.dot(grad_b0, w_point[0], preferred_element_type=f32))
    grad_conv0 = (
        grad_second0 * snake_slope(conv0[skip : skip + rows_back], freq_point[0])
    ).astype(bf16)

    def dil_gradient(grad_conv, extent, spacing, inputs):
        rows = grad_conv.shape[0]
        mine = exchange(grad_conv.T.reshape(quad, width, rows), QUAD)
        parts = []
        for q in range(quad):
            masks = tap_masks(0, spacing, -1, (tm_index * quad + q) * slot)
            row = []
            for tap in range(taps):
                begin = extent - spacing * (tap - 3)
                part = mine[q, :, begin : begin + slot]
                row.append(jnp.where(masks[tap][None, :], part, jnp.zeros((), bf16)))
            parts.append(jnp.concatenate(row, axis=0))
        left = jnp.concatenate(parts, axis=1)
        return jnp.dot(left, inputs, preferred_element_type=f32).astype(bf16)

    def over_time(value):
        rows = value.shape[0]
        arrived = exchange(value.reshape(tm_size, rows // tm_size, channels), TM)
        total = natural(arrived.astype(f32).sum(axis=0).astype(bf16))
        return copies(total, TM).reshape(rows, channels)

    def point_gradient(grad_b, second):
        partial = lax.dot_general(
            grad_b, second, (((0,), (0,)), ((), ())), preferred_element_type=f32
        ).astype(bf16)
        arrived = exchange(partial.reshape(quad, width, channels), QUAD)
        return arrived.astype(f32).sum(axis=0).astype(bf16)

    inputs0 = over_quad(first0_all[EXT_UP : EXT_UP + slot], 0).reshape(quad * slot, channels)
    inputs1 = over_quad(first1_all[EXT_MID : EXT_MID + slot], 0).reshape(quad * slot, channels)
    wide_gc1 = grad_conv1[EXT_GRAD - EXT_MID : EXT_GRAD + slot + EXT_MID]
    dil1 = dil_gradient(wide_gc1, EXT_MID, 9, inputs1)
    point1 = point_gradient(cot, second1_all)
    total1 = over_time(jnp.concatenate([dil1, point1]))
    point0 = point_gradient(
        grad_b0[EXT_BACK : EXT_BACK + slot], second0_all[EXT_MID : EXT_MID + slot]
    )
    dil0 = dil_gradient(grad_conv0, EXT_BACK, 3, inputs0)
    dil0, total1 = lax.optimization_barrier((dil0, total1))
    total0 = over_time(jnp.concatenate([dil0, point0]))
    cut = taps * width
    dil_total = jnp.stack([total0[:cut], total1[:cut]]).reshape(units, taps, width, channels)
    point_total = jnp.stack([total0[cut:], total1[cut:]])
    return (
        decoded,
        dil_eff.astype(f32) * dil_total.astype(f32),
        point_eff.astype(f32) * point_total.astype(f32),
    )


def solution(mesh):
    fine = Mesh(mesh.devices.reshape(4, 4, 2, 8, 2), ("x", "yh", "yl", "z", "k"))
    return jax.shard_map(
        per_device,
        mesh=fine,
        in_specs=(
            P(CHAN, TM),
            P(None, CHAN, TM),
            P(None, None, CHAN, None),
            P(None, CHAN, None),
            P(None, None, CHAN, None),
            P(None, CHAN, None),
            P(CHAN),
            P(None, CHAN),
            P(None, CHAN),
            P(),
            P(CHAN, TM),
        ),
        out_specs=(P(CHAN, TM), P(None, None, CHAN, None), P(None, CHAN, None)),
        check_vma=False,
    )
```

```python
import jax
import jax.numpy as jnp
from jax import lax
from jax.experimental import pallas as pl
from jax.experimental.pallas import tpu as pltpu
from jax.sharding import Mesh, PartitionSpec as P

TM = ("x", "yh")
CHAN = ("yl", "z", "k")
QUAD = ("yl", "k")
SLOT = ("x", "yh", "yl", "k")
EDGE = 6
EXT_UP = 48
EXT_MID = 32
EXT_GRAD = 48
EXT_BACK = 16
f32 = jnp.float32
bf16 = jnp.bfloat16
i32 = jnp.int32


def exchange(pieces, axes):
    return lax.all_to_all(pieces, axes, 0, 0, tiled=True)


def copies(value, axes):
    size = lax.axis_size(axes)
    return exchange(jnp.broadcast_to(value[None], (size, *value.shape)), axes)


def shift_pairs(axes, step):
    size = lax.axis_size(axes)
    return [(i, i + step) for i in range(size) if 0 <= i + step < size]


def from_before(value, axes):
    return lax.ppermute(value, axes, shift_pairs(axes, 1))


def from_after(value, axes):
    return lax.ppermute(value, axes, shift_pairs(axes, -1))


def snake_act(values, alpha):
    return values + jnp.sin(alpha * values) ** 2 / alpha


def snake_slope(values, alpha):
    return 1.0 + jnp.sin(2.0 * alpha * values)


def swapped(value, name):
    return lax.ppermute(value, name, [(0, 1), (1, 0)])


def paired(mine, other, name, axis):
    pick = (jnp.arange(2, dtype=i32) == lax.axis_index(name)).reshape(
        (1,) * axis + (2,) + (1,) * (mine.ndim - axis)
    )
    return jnp.where(pick, jnp.expand_dims(mine, axis), jnp.expand_dims(other, axis))


def over_quad(value, axis):
    pair = paired(value, swapped(value, "yl"), "yl", axis)
    out = paired(pair, swapped(pair, "k"), "k", axis + 1)
    return out.reshape(*value.shape[:axis], -1, *value.shape[axis:])


def halves(value, name, axis):
    index = lax.axis_index(name)
    keep = lax.dynamic_index_in_dim(value, index, axis, keepdims=False)
    give = lax.dynamic_index_in_dim(value, 1 - index, axis, keepdims=False)
    return keep, swapped(give, name)


def quad_exchange(pieces):
    pieces = pieces.reshape(2, 2, *pieces.shape[1:])
    keep, got = halves(pieces, "yl", 0)
    pieces = paired(keep, got, "yl", 0)
    keep, got = halves(pieces, "k", 1)
    pieces = paired(keep, got, "k", 1)
    return pieces.reshape(4, *pieces.shape[2:])


def quad_sum(pieces):
    pieces = pieces.reshape(2, 2, *pieces.shape[1:])
    keep, got = halves(pieces, "yl", 0)
    pieces = (keep.astype(f32) + got.astype(f32)).astype(bf16)
    keep, got = halves(pieces, "k", 0)
    return (keep.astype(f32) + got.astype(f32)).astype(bf16)


def call(body, outs, *args, scalars=0, scratch=(), name=None):
    smem = [pl.BlockSpec(memory_space=pltpu.SMEM)] * scalars
    vmem = [pl.BlockSpec(memory_space=pltpu.VMEM)] * (len(args) - scalars)
    return pl.pallas_call(
        body,
        out_shape=[jax.ShapeDtypeStruct(shape, dtype) for shape, dtype in outs],
        in_specs=smem + vmem,
        out_specs=[pl.BlockSpec(memory_space=pltpu.VMEM)] * len(outs),
        scratch_shapes=[pltpu.VMEM(shape, dtype) for shape, dtype in scratch],
        name=name,
    )(*args)


def nt(a, b):
    return lax.dot_general(a, b, (((1,), (1,)), ((), ())), preferred_element_type=f32)


def nn(a, b):
    return lax.dot_general(a, b, (((1,), (0,)), ((), ())), preferred_element_type=f32)


def per_device(
    latent_input,
    upsample_kernel,
    dilated_kernel,
    pointwise_kernel,
    dilated_prune_mask,
    pointwise_prune_mask,
    snake_freq_upsample,
    snake_freq_dilated,
    snake_freq_pointwise,
    segment_lengths,
    cotangent,
):
    taps2, width, cols = upsample_kernel.shape
    stride = taps2 // 2
    shift = stride.bit_length() - 1
    frames = latent_input.shape[1]
    tm_size = lax.axis_size(TM)
    x_size = lax.axis_size("x")
    yh_size = lax.axis_size("yh")
    quad = lax.axis_size(QUAD)
    z_size = lax.axis_size("z")
    y_size = lax.axis_size("yl")
    total_frames = frames * tm_size
    slot_latent = frames // quad
    slot = slot_latent * stride
    units, taps, _, channels = dilated_kernel.shape
    block = quad * width
    segments = segment_lengths.shape[0]
    pos = (lax.axis_index(TM) * quad + lax.axis_index(QUAD)).astype(i32).reshape(1)

    def ids_of(lens, latent):
        found = jnp.full(latent.shape, -1, i32)
        start = 0
        for s in range(segments):
            found = found + (latent >= start).astype(i32)
            start = start + lens[s]
        return jnp.where(latent < 0, -1, jnp.where(latent >= total_frames, -2, found))

    def same_track(lens, rows, offset):
        own = ids_of(lens, lax.shift_right_arithmetic(rows, shift))
        return own == ids_of(lens, lax.shift_right_arithmetic(rows + offset, shift))

    cot_pieces = exchange(cotangent.reshape(width, quad, slot).transpose(1, 0, 2), QUAD)
    margin = (128 - frames) // 2
    span = frames + 2 * margin
    latent_before = from_before(latent_input[:, -margin:], TM)
    latent_after = from_after(latent_input[:, :margin], TM)
    kernel_own = upsample_kernel.reshape(taps2 * width, cols)
    kernel_parts = [kernel_own]
    for step in range(1, yh_size):
        kernel_parts.append(
            lax.ppermute(
                kernel_own, "yh", [(i, (i + step) % yh_size) for i in range(yh_size)]
            )
        )
    wide = jnp.concatenate([latent_before, latent_input, latent_after], axis=1)
    wide = snake_act(wide.astype(f32), snake_freq_upsample[:, None]).astype(bf16)
    inputs_all = copies(wide, CHAN)
    inputs_x = exchange(inputs_all.reshape(x_size, -1, span), "x")

    def pruned(kernel, mask):
        lanes = mask.shape[-1]
        group = jnp.arange(channels, dtype=i32) // (channels // lanes)
        expand = (jnp.arange(lanes, dtype=i32)[:, None] == group[None, :]).astype(bf16)
        rows = mask.astype(bf16).reshape(-1, lanes)
        wide_mask = jnp.dot(rows, expand, preferred_element_type=f32).astype(bf16)
        return (kernel.reshape(-1, channels) * wide_mask).reshape(kernel.shape)

    lane = jnp.arange(channels, dtype=i32)
    part = channels // (z_size * y_size)
    source = (lane // part) % y_size * (z_size * part) + lane // (y_size * part) * part + lane % part
    reorder = (lane[:, None] == source[None, :]).astype(bf16)

    def z_first(value):
        moved = jnp.dot(value.reshape(-1, channels), reorder, preferred_element_type=f32)
        return moved.astype(bf16).reshape(value.shape)

    dil_eff = pruned(dilated_kernel, dilated_prune_mask)
    point_eff = pruned(pointwise_kernel, pointwise_prune_mask)
    early = z_first(jnp.concatenate([point_eff, dil_eff[0]], axis=0))
    early = over_quad(early, 1).reshape((units + taps) * block, channels)
    w_point = [early[u * block : (u + 1) * block] for u in range(units)]
    w_dil = [early[units * block :]]
    w_dil.append(over_quad(z_first(dil_eff[1]), 1).reshape(taps * block, channels))
    cot = cot_pieces.reshape(block, slot).T

    freqs = jnp.concatenate([snake_freq_dilated, snake_freq_pointwise]).reshape(1, -1)
    freqs = jnp.pad(freqs, ((0, 0), (0, stride * width - freqs.shape[1])))
    thirds = []
    for _ in range(3):
        thirds.append(lax.reduce_precision(freqs, 8, 7))
        freqs = freqs - thirds[-1]
    thirds = jnp.pad(jnp.concatenate(thirds), ((0, 5), (0, 0))).astype(bf16)
    half = stride // 2 * width
    wide_latent = slot_latent + 2 * EDGE
    piece_rows = wide_latent + 8

    def pieces_body(pos, lens, xs, w0, w1, w2, w3, thirds, out, mixed):
        yh = (pos[0] // quad) % yh_size
        for xi in range(x_size):
            total = jnp.zeros((taps2 * width, span), f32)
            for step, w in enumerate((w0, w1, w2, w3)):
                begin = pl.multiple_of((yh + yh_size - step) % yh_size * cols, cols)
                total = total + nn(w[...], xs[xi, pl.ds(begin, cols), :])
            mixed[...] = total.T
            first_latent = (xi * yh_size + yh) * frames - EDGE
            for q in range(quad):
                row = margin - EDGE + q * slot_latent
                lat = (
                    first_latent
                    + q * slot_latent
                    + lax.broadcasted_iota(i32, (wide_latent, half), 0)
                )
                here = ids_of(lens, lat)
                prev_ok = here == ids_of(lens, lat - 1)
                next_ok = here == ids_of(lens, lat + 1)
                lower = mixed[row - 1 : row - 1 + wide_latent, 3 * half :]
                upper = mixed[row + 1 : row + 1 + wide_latent, :half]
                low = mixed[row : row + wide_latent, half : 2 * half]
                high = mixed[row : row + wide_latent, 2 * half : 3 * half]
                low = low + jnp.where(prev_ok, lower, 0.0)
                high = high + jnp.where(next_ok, upper, 0.0)
                out[xi * quad + q, :wide_latent, :half] = low.astype(bf16)
                out[xi * quad + q, :wide_latent, half:] = high.astype(bf16)
                out[xi * quad + q, wide_latent:, :] = thirds[...]

    (pieces,) = call(
        pieces_body,
        [((x_size * quad, piece_rows, stride * width), bf16)],
        pos,
        segment_lengths,
        inputs_x,
        *kernel_parts,
        thirds,
        scalars=2,
        scratch=[((span, taps2 * width), f32)],
        name="up_pieces",
    )
    arrived = exchange(pieces, ("x", "yl", "k"))

    rows_up = slot + 2 * EXT_UP
    rows_mid = slot + 2 * EXT_MID
    rows_back = slot + 2 * EXT_BACK
    rows_grad = slot + 2 * EXT_GRAD

    def input_body(arr, cot, w, hidden, payload, freqs):
        sums = []
        for q in range(quad):
            total = arr[q].astype(f32)
            for xi in range(1, x_size):
                total = total + arr[xi * quad + q].astype(f32)
            sums.append(total)
        for p in range(stride):
            row = jnp.concatenate(
                [s[:wide_latent, p * width : (p + 1) * width] for s in sums], axis=1
            )
            hidden[pl.ds(p, wide_latent, stride=stride), :] = row
        marks = [
            arr[q, wide_latent:, :].astype(f32).sum(axis=0, keepdims=True) for q in range(quad)
        ]
        for u in range(2 * units):
            freqs[u : u + 1, :] = jnp.concatenate(
                [m[:, u * width : (u + 1) * width] for m in marks], axis=1
            )
        first = snake_act(hidden[...], freqs[0:1, :]).astype(bf16)
        partial = nn(cot[...], w[...]).astype(bf16)
        for z in range(z_size):
            payload[z, :rows_up, :] = first
            payload[z, rows_up:, :] = partial[:, z * block : (z + 1) * block]

    hidden, payload, freqs = call(
        input_body,
        [
            ((rows_up, block), f32),
            ((z_size, rows_up + slot, block), bf16),
            ((2 * units, block), f32),
        ],
        arrived,
        cot,
        w_point[1],
        name="unit0_input",
    )
    first0 = exchange(payload, "z")

    def conv(arr, w, lens, start, joined, full, rows_in, rows_out, spacing, extent_gap, begin_time):
        for z in range(z_size):
            joined[:, z * block : (z + 1) * block] = arr[z, :rows_in, :]
        full[...] = nt(joined[...], w[...])
        rows = begin_time + lax.broadcasted_iota(i32, (rows_out, block), 0)
        total = jnp.zeros((rows_out, block), f32)
        for tap in range(taps):
            offset = (tap - 3) * spacing
            begin = extent_gap + offset
            part = full[begin : begin + rows_out, tap * block : (tap + 1) * block]
            total = total + jnp.where(same_track(lens, rows, offset), part, 0.0)
        return total

    def conv0_body(pos, lens, arr, w, freqs, conv_out, payload, own, grad, joined, full):
        start = pos[0] * slot
        total = conv(
            arr, w, lens, start, joined, full, rows_up, rows_mid, 3, EXT_UP - EXT_MID,
            start - EXT_MID,
        )
        conv_out[...] = total
        second = snake_act(total, freqs[units : units + 1, :]).astype(bf16)
        for z in range(z_size):
            payload[z] = second
        own[...] = joined[EXT_UP : EXT_UP + slot, :]
        partial = arr[0, rows_up:, :].astype(f32)
        for z in range(1, z_size):
            partial = partial + arr[z, rows_up:, :].astype(f32)
        grad[...] = partial

    conv0, payload, own0, grad_second1 = call(
        conv0_body,
        [
            ((rows_mid, block), f32),
            ((z_size, rows_mid, block), bf16),
            ((slot, channels), bf16),
            ((slot, block), f32),
        ],
        pos,
        segment_lengths,
        first0,
        w_dil[0],
        freqs,
        scalars=2,
        scratch=[((rows_up, channels), bf16), ((rows_up, taps * block), f32)],
        name="unit0_conv",
    )
    second0 = exchange(payload, "z")

    def point0_body(arr, w, hidden, freqs, hidden_out, payload, joined):
        for z in range(z_size):
            joined[:, z * block : (z + 1) * block] = arr[z]
        gap = EXT_UP - EXT_MID
        total = hidden[gap : gap + rows_mid, :] + nt(joined[...], w[...])
        hidden_out[...] = total
        first = snake_act(total, freqs[1:2, :]).astype(bf16)
        for z in range(z_size):
            payload[z] = first

    hidden1, payload = call(
        point0_body,
        [((rows_mid, block), f32), ((z_size, rows_mid, block), bf16)],
        second0,
        w_point[0],
        hidden,
        freqs,
        scratch=[((rows_mid, channels), bf16)],
        name="unit0_point",
    )
    first1 = exchange(payload, "z")

    def conv1_body(
        pos, lens, arr, w, freqs, grad, cot, second, grad_conv, to_after, to_before, own, joined, full
    ):
        start = pos[0] * slot
        total = conv(
            arr, w, lens, start, joined, full, rows_mid, slot, 9, EXT_MID, start
        )
        alpha = freqs[units + 1 : units + 2, :]
        second[...] = snake_act(total, alpha).astype(bf16)
        result = (grad[...] * snake_slope(total, alpha)).astype(bf16)
        grad_conv[...] = result
        to_after[:EXT_GRAD, :] = result[slot - EXT_GRAD :, :]
        to_after[EXT_GRAD:, :] = cot[slot - EXT_BACK :, :]
        to_before[:EXT_GRAD, :] = result[:EXT_GRAD, :]
        to_before[EXT_GRAD:, :] = cot[:EXT_BACK, :]
        own[...] = joined[EXT_MID : EXT_MID + slot, :]

    second1, grad_conv1, to_after, to_before, own1 = call(
        conv1_body,
        [
            ((slot, block), bf16),
            ((slot, block), bf16),
            ((EXT_GRAD + EXT_BACK, block), bf16),
            ((EXT_GRAD + EXT_BACK, block), bf16),
            ((slot, channels), bf16),
        ],
        pos,
        segment_lengths,
        first1,
        w_dil[1],
        freqs,
        grad_second1,
        cot,
        scalars=2,
        scratch=[((rows_mid, channels), bf16), ((rows_mid, taps * block), f32)],
        name="unit1_conv",
    )
    before = from_before(to_after, SLOT)
    after = from_after(to_before, SLOT)

    def dgrad_body(
        pos, lens, grad, before, after, second, cot, w, payload, turned, cot_wide, whole, windows
    ):
        whole[:EXT_GRAD, :] = before[:EXT_GRAD, :].astype(f32)
        whole[EXT_GRAD : EXT_GRAD + slot, :] = grad[...].astype(f32)
        whole[EXT_GRAD + slot :, :] = after[:EXT_GRAD, :].astype(f32)
        cot_wide[:EXT_BACK, :] = before[EXT_GRAD:, :]
        cot_wide[EXT_BACK : EXT_BACK + slot, :] = cot[...]
        cot_wide[EXT_BACK + slot :, :] = after[EXT_GRAD:, :]
        rows = pos[0] * slot - EXT_BACK + lax.broadcasted_iota(i32, (rows_back, block), 0)
        for tap in range(taps):
            offset = (tap - 3) * 9
            begin = EXT_GRAD - EXT_BACK - offset
            part = whole[begin : begin + rows_back, :]
            part = jnp.where(same_track(lens, rows, -offset), part, 0.0)
            windows[:, tap * block : (tap + 1) * block] = part.astype(bf16)
        partial = nn(windows[...], w[...]).astype(bf16)
        for z in range(z_size):
            payload[z, :rows_back, :] = partial[:, z * block : (z + 1) * block]
            payload[z, rows_back:, :] = second[...]
        flat = whole[...].T.astype(bf16)
        for q in range(quad):
            turned[q] = flat[q * width : (q + 1) * width, :]

    payload, turned1, cot_wide = call(
        dgrad_body,
        [
            ((z_size, rows_back + slot, block), bf16),
            ((quad, width, rows_grad), bf16),
            ((rows_back, block), bf16),
        ],
        pos,
        segment_lengths,
        grad_conv1,
        before,
        after,
        second1,
        cot,
        w_dil[1],
        scalars=2,
        scratch=[((rows_grad, block), f32), ((rows_back, taps * block), bf16)],
        name="unit1_dgrad",
    )
    mixed1 = exchange(payload, "z")

    def grad0_body(arr, hidden, freqs, cot, w, grad_b, payload):
        total = arr[0, :rows_back, :].astype(f32)
        for z in range(1, z_size):
            total = total + arr[z, :rows_back, :].astype(f32)
        skip = EXT_MID - EXT_BACK
        slope = snake_slope(hidden[skip : skip + rows_back, :], freqs[1:2, :])
        result = (cot[...].astype(f32) + total * slope).astype(bf16)
        grad_b[...] = result
        partial = nn(result, w[...]).astype(bf16)
        for z in range(z_size):
            payload[z] = partial[:, z * block : (z + 1) * block]

    grad_b0, payload = call(
        grad0_body,
        [((rows_back, block), bf16), ((z_size, rows_back, block), bf16)],
        mixed1,
        hidden1,
        freqs,
        cot_wide,
        w_point[0],
        name="unit0_grad",
    )
    parts0 = exchange(payload, "z")

    def turn0_body(arr, conv, freqs, turned, whole):
        total = arr[0].astype(f32)
        for z in range(1, z_size):
            total = total + arr[z].astype(f32)
        skip = EXT_MID - EXT_BACK
        slope = snake_slope(conv[skip : skip + rows_back, :], freqs[units : units + 1, :])
        whole[:rows_back, :] = total * slope
        whole[rows_back:, :] = jnp.zeros((rows_grad - rows_back, block), f32)
        flat = whole[...].T.astype(bf16)
        for q in range(quad):
            turned[q] = flat[q * width : (q + 1) * width, :]

    (turned0,) = call(
        turn0_body,
        [((quad, width, rows_grad), bf16)],
        parts0,
        conv0,
        freqs,
        scratch=[((rows_grad, block), f32)],
        name="unit0_turn",
    )

    def weight_sums(pos, lens, arr, inputs, windows, spacing, extent):
        total = jnp.zeros((taps * width, channels), f32)
        column = lax.broadcasted_iota(i32, (width, rows_grad), 1)
        for q in range(quad):
            turned = arr[q].astype(f32)
            rows = (pos[0] // quad * quad + q) * slot + column
            for tap in range(taps):
                offset = (tap - 3) * spacing
                begin = extent - offset
                part = pltpu.roll(turned, rows_grad - begin, 1)
                keep = jnp.logical_and(same_track(lens, rows, -offset), column < slot)
                windows[tap * width : (tap + 1) * width, :] = jnp.where(keep, part, 0.0).astype(
                    bf16
                )
            total = total + nn(windows[:, :slot], inputs[q])
        return total.astype(bf16)

    def dil1_body(pos, lens, arr, inputs, out, windows):
        out[...] = weight_sums(pos, lens, arr, inputs, windows, 9, EXT_GRAD)

    cut = taps * width
    per_owner = (taps + 1) * width // tm_size

    def dil0_body(pos, lens, arr, inputs, dil1, points, out, windows):
        total = weight_sums(pos, lens, arr, inputs, windows, 3, EXT_BACK)
        for m in range(tm_size):
            row = m * per_owner
            if row < cut:
                out[m, :per_owner, :] = total[row : row + per_owner, :]
                out[m, per_owner:, :] = dil1[row : row + per_owner, :]
            else:
                out[m, :per_owner, :] = points[0, row - cut : row - cut + per_owner, :]
                out[m, per_owner:, :] = points[1, row - cut : row - cut + per_owner, :]

    inputs0 = over_quad(own0, 0)
    inputs1 = over_quad(own1, 0)
    window_scratch = [((taps * width, rows_grad), bf16)]
    (dil1,) = call(
        dil1_body,
        [((cut, channels), bf16)],
        pos,
        segment_lengths,
        quad_exchange(turned1),
        inputs1,
        scalars=2,
        scratch=window_scratch,
        name="dil1_sums",
    )
    second1_all = mixed1[:, rows_back:].transpose(1, 0, 2).reshape(slot, channels)
    second0_all = (
        second0[:, EXT_MID : EXT_MID + slot].transpose(1, 0, 2).reshape(slot, channels)
    )
    decoded_block = hidden1[EXT_MID : EXT_MID + slot] + nt(second1_all, w_point[1])
    decoded = (
        quad_exchange(decoded_block.astype(bf16).T.reshape(quad, width, slot))
        .transpose(1, 0, 2)
        .reshape(width, quad * slot)
    )

    def point_gradient(grad_b, second):
        return lax.dot_general(
            grad_b, second, (((0,), (0,)), ((), ())), preferred_element_type=f32
        ).astype(bf16)

    points = jnp.stack(
        [
            point_gradient(grad_b0[EXT_BACK : EXT_BACK + slot], second0_all).reshape(
                quad, width, channels
            ),
            point_gradient(cot, second1_all).reshape(quad, width, channels),
        ],
        axis=1,
    )
    points = quad_sum(points)

    (sums,) = call(
        dil0_body,
        [((tm_size, 2 * per_owner, channels), bf16)],
        pos,
        segment_lengths,
        exchange(turned0, QUAD),
        inputs0,
        dil1,
        points,
        scalars=2,
        scratch=window_scratch,
        name="dil0_sums",
    )
    sums = exchange(sums, TM)

    def owner_body(arr, out):
        total = arr[0].astype(f32)
        for m in range(1, tm_size):
            total = total + arr[m].astype(f32)
        columns = []
        for y in range(y_size):
            for z in range(z_size):
                begin = (z * y_size + y) * part
                columns.append(total[:, begin : begin + part])
        total = jnp.concatenate(columns, axis=1).astype(bf16)
        for m in range(tm_size):
            out[m] = total

    (sums,) = call(
        owner_body, [((tm_size, 2 * per_owner, channels), bf16)], sums, name="owner_sums"
    )
    sums = exchange(sums, TM)

    def final_body(arr, dil, point, dil_out, point_out):
        for u in range(units):
            for m in range(tm_size):
                row = m * per_owner
                value = arr[m, u * per_owner : (u + 1) * per_owner, :].astype(f32)
                inner = row % width
                if row < cut:
                    weight = dil[u, row // width, inner : inner + per_owner, :].astype(f32)
                    dil_out[u, row // width, inner : inner + per_owner, :] = weight * value
                else:
                    weight = point[u, inner : inner + per_owner, :].astype(f32)
                    point_out[u, inner : inner + per_owner, :] = weight * value

    dil_saliency, point_saliency = call(
        final_body,
        [((units, taps, width, channels), f32), ((units, width, channels), f32)],
        sums,
        dil_eff,
        point_eff,
        name="saliency",
    )
    return decoded, dil_saliency, point_saliency


def solution(mesh):
    fine = Mesh(mesh.devices.reshape(4, 4, 2, 8, 2), ("x", "yh", "yl", "z", "k"))
    return jax.shard_map(
        per_device,
        mesh=fine,
        in_specs=(
            P(CHAN, TM),
            P(None, CHAN, TM),
            P(None, None, CHAN, None),
            P(None, CHAN, None),
            P(None, None, CHAN, None),
            P(None, CHAN, None),
            P(CHAN),
            P(None, CHAN),
            P(None, CHAN),
            P(),
            P(CHAN, TM),
        ),
        out_specs=(P(CHAN, TM), P(None, None, CHAN, None), P(None, CHAN, None)),
        check_vma=False,
    )
```
